256 devices in a mesh: hi: 16 (over z, core), lo: 16 (over x, y).
Axes of the slice: x: 4, y: 4, z: 8, core: 2. Of those that a mesh axis runs over, the one named last changes fastest.
Arguments:
- points: float32 [3, 1024, 512], P(None, ('hi', 'lo')), as said below
- solution: float32 [16, 1024, 512], P(None, ('hi', 'lo')), may hold values from -6 to 6
- residual: float32 [16, 1024, 512], P(None, ('hi', 'lo')), may hold values from -300 to 300
- direction: float32 [16, 1024, 512], P(None, ('hi', 'lo')), may hold values from -300 to 300
- nugget: float32 [1024, 512], P(('hi', 'lo')), may hold values from 0.5 to 2
- leaf_basis: float32 [1024, 512, 128], P(('hi', 'lo')), may hold values from -0.25 to 0.25
- transfer: float32 [1024, 128, 128], P(('hi', 'lo')), may hold values from -0.5 to 0.5
- far_coupling: float32 [1024, 16, 128, 128], P(('hi', 'lo')), may hold values from -0.125 to 0.125
- coarse_up: float32 [256, 8, 128, 128], P(('hi', 'lo')), may hold values from -0.5 to 0.5
- coarse_down: float32 [256, 8, 128, 128], P(('hi', 'lo')), may hold values from -0.5 to 0.5
- near_ids: int32 [1024, 27], P(('hi', 'lo')), may hold values from 0 to 1023, as said below
- near_count: int32 [1024], P(('hi', 'lo')), may hold values from 1 to 27, as said below
- far_ids: int32 [1024, 16], P(('hi', 'lo')), may hold values from 0 to 1023, as said below
Outputs:
- new_solution: float32 [16, 1024, 512], P(None, ('hi', 'lo'))
- new_residual: float32 [16, 1024, 512], P(None, ('hi', 'lo'))
- new_direction: float32 [16, 1024, 512], P(None, ('hi', 'lo'))
The draws below stay inside these ranges and needn't reach their ends.
Inputs may be any that keep to these rules, and one draw needn't show every extreme that they name: The points of leaf i lie in the cube of side 3 centred on the unit Morton cell of i, that cell read from the bits of i in x, y, z order from the lowest bit. `near_ids`: row i starts with i itself; every entry of row i lies in the aligned block of 64 leaves that holds i; entries from slot near_count[i] on are not used. `near_count`: some leaf uses all 27 slots. `far_ids`: every entry of row i lies in the aligned block of 64 leaves that holds i.
All inputs are finite; a program needn't handle non-finite values.
Results may differ from the reference program's by a relative error of at most 0.0003.
Values sent between devices are 32-bit elements; how exact they have to be, the bound alone decides.
A program may use at most 128 MiB of HBM per device.

```python
import math
import jax
import jax.numpy as jnp
from jax import lax

LEAF_SIZE = 512
RANK = 128
PROBES = 16
NEAR_SLOTS = 27
FAR_SLOTS = 16
LEAF_DEV = 4
BOXES = 256
LEAVES = 1024
GROUP_LEAVES = 64
LEVELS = 8


def draw_points(key, part):
    offset_key = jax.random.fold_in(key, 17)
    leaf_index = jnp.arange(LEAVES, dtype=jnp.int32)
    cells = [jnp.zeros((LEAVES,), jnp.int32), jnp.zeros((LEAVES,), jnp.int32), jnp.zeros((LEAVES,), jnp.int32)]
    for bit in range(LEAVES.bit_length() - 1):
        digit = leaf_index >> bit & 1
        cells[bit % 3] = cells[bit % 3] + digit * (1 << bit // 3)
    corner = jnp.stack(cells, axis=0).astype(jnp.float32)
    inside = jax.random.uniform(offset_key, (3, LEAVES, LEAF_SIZE), jnp.float32)
    return (corner[:, :, None] - 1.0 + 3.0 * inside).astype(jnp.float32)


def scaled_vector(key):
    normal_key = jax.random.fold_in(key, 0)
    raw_values = jnp.clip(jax.random.normal(normal_key, (PROBES, LEAVES, LEAF_SIZE), jnp.float32), -6.0, 6.0)
    leaf_share = jnp.arange(LEAVES, dtype=jnp.float32) / max(LEAVES - 1, 1)
    probe_share = jnp.arange(PROBES, dtype=jnp.float32) / max(PROBES - 1, 1)
    scaling = jnp.exp(math.log(3.0) * leaf_share)[None, :, None] * jnp.exp(math.log(10.0) * probe_share)[:, None, None] / 3.0
    return (raw_values * scaling).astype(jnp.float32)


def draw_residual(key, part):
    return scaled_vector(jax.random.fold_in(key, 3))


def draw_direction(key, part):
    return scaled_vector(jax.random.fold_in(key, 5))


def neighbour_offsets(key):
    others = GROUP_LEAVES - 1
    scores = jax.random.randint(jax.random.fold_in(key, 7), (LEAVES, others), 0, 1 << 20) * others + jnp.arange(others, dtype=jnp.int32)[None, :]
    return jnp.argsort(scores, axis=1, stable=True).astype(jnp.int32) + 1


def leaf_targets(offsets):
    leaf_index = jnp.arange(LEAVES, dtype=jnp.int32)[:, None]
    block_start = leaf_index // GROUP_LEAVES * GROUP_LEAVES
    position = leaf_index % GROUP_LEAVES
    return (block_start + (position + offsets) % GROUP_LEAVES).astype(jnp.int32)


def draw_near_ids(key, part):
    offsets = neighbour_offsets(key)
    others = GROUP_LEAVES - 1
    columns = jnp.arange(NEAR_SLOTS - 1, dtype=jnp.int32) % others
    chosen = leaf_targets(offsets[:, columns])
    itself = jnp.arange(LEAVES, dtype=jnp.int32)[:, None]
    return jnp.concatenate([itself, chosen], axis=1).astype(jnp.int32)


def draw_far_ids(key, part):
    offsets = neighbour_offsets(key)
    others = GROUP_LEAVES - 1
    columns = (NEAR_SLOTS - 1 + jnp.arange(FAR_SLOTS, dtype=jnp.int32)) % others
    return leaf_targets(offsets[:, columns])


def draw_near_count(key, part):
    dense_key, count_key, forced_key = jax.random.split(jax.random.fold_in(key, 13), 3)
    density = jax.random.randint(dense_key, (BOXES,), 1, NEAR_SLOTS + 1)
    per_leaf = jnp.repeat(density, LEAF_DEV)
    counts = jax.random.randint(count_key, (LEAVES,), 1, per_leaf + 1)
    forced = jax.random.randint(forced_key, (), 0, LEAVES)
    counts = jnp.where(jnp.arange(LEAVES, dtype=jnp.int32) == forced, NEAR_SLOTS, counts)
    return counts.astype(jnp.int32)


def block_levels(key, shape, pieces, smallest, largest):
    level = 1.0
    for dim, shards_of in pieces:
        draws = jax.random.uniform(jax.random.fold_in(jax.random.fold_in(key, 6), dim), (shards_of,), jnp.float32, smallest / len(pieces), largest / len(pieces))
        level = level * jnp.repeat(jnp.exp(draws), shape[dim] // shards_of).reshape((-1,) + (1,) * (len(shape) - 1 - dim))
    return level


def gaussian(rng, dims, scale, most, cuts=(), held_as=jnp.bfloat16):
    array = scale * jax.random.normal(rng, dims, jnp.float32)
    if cuts:
        array = array * block_levels(rng, dims, cuts, -0.22, 0.18)
    return jnp.clip(array, -most, most).astype(held_as)


def setup_inputs(seed: int = 0) -> dict:
    arg_keys = jax.random.split(jax.random.key(seed), 14)
    points = draw_points(jax.random.fold_in(arg_keys[13], 71), 0)
    solution = gaussian(arg_keys[1], (PROBES, LEAVES, LEAF_SIZE), 1.0, 6.0, ((1, 256),), jnp.float32)
    residual = draw_residual(jax.random.fold_in(arg_keys[13], 71), 0)
    direction = draw_direction(jax.random.fold_in(arg_keys[13], 71), 0)
    nugget = jnp.clip(jnp.exp(math.log(2.0) - 1.3862944 * jax.random.uniform(arg_keys[4], (LEAVES, LEAF_SIZE), jnp.float32) ** block_levels(arg_keys[4], (LEAVES, LEAF_SIZE), ((0, 256),), -0.2, 0.2)), 0.5, 2.0)
    leaf_basis = gaussian(arg_keys[5], (LEAVES, LEAF_SIZE, RANK), LEAF_SIZE ** -0.5, 0.25, ((0, 256),), jnp.float32)
    transfer = gaussian(arg_keys[6], (LEAVES, RANK, RANK), RANK ** -0.5, 0.5, ((0, 256),), jnp.float32)
    far_coupling = gaussian(arg_keys[7], (LEAVES, FAR_SLOTS, RANK, RANK), (RANK * FAR_SLOTS) ** -0.5, 0.125, ((0, 256),), jnp.float32)
    coarse_up = gaussian(arg_keys[8], (BOXES, LEVELS, RANK, RANK), RANK ** -0.5, 0.5, ((0, 256),), jnp.float32)
    coarse_down = gaussian(arg_keys[9], (BOXES, LEVELS, RANK, RANK), RANK ** -0.5, 0.5, ((0, 256),), jnp.float32)
    near_ids = draw_near_ids(jax.random.fold_in(arg_keys[13], 71), 0)
    near_count = draw_near_count(jax.random.fold_in(arg_keys[13], 71), 0)
    far_ids = draw_far_ids(jax.random.fold_in(arg_keys[13], 71), 0)
    return dict(points=points, solution=solution, residual=residual, direction=direction, nugget=nugget, leaf_basis=leaf_basis, transfer=transfer, far_coupling=far_coupling, coarse_up=coarse_up, coarse_down=coarse_down, near_ids=near_ids, near_count=near_count, far_ids=far_ids)


length_scale = 1.0
root_three = math.sqrt(3.0)
epsilon = 1e-06
highest = lax.Precision.HIGHEST

def matern_block(target_points, source_points):
    squared = jnp.zeros((target_points.shape[1], target_points.shape[2], source_points.shape[2]), jnp.float32)
    for coord in range(3):
        gap = target_points[coord][:, :, None] - source_points[coord][:, None, :]
        squared = squared + gap * gap
    scaled = root_three / length_scale * jnp.sqrt(squared)
    return (1.0 + scaled) * jnp.exp(-scaled)

def near_field(points, direction, near_ids, near_count):
    width = math.gcd(LEAVES, 16)
    blocks = LEAVES // width
    point_blocks = points.reshape(3, blocks, width, LEAF_SIZE).transpose(1, 0, 2, 3)
    id_blocks = near_ids.reshape(blocks, width, NEAR_SLOTS)
    count_blocks = near_count.reshape(blocks, width)

    def one_block(items):
        target_points, block_ids, block_counts = items

        def one_slot(total, slot_index):
            source = block_ids[:, slot_index]
            source_points = jnp.take(points, source, axis=1)
            kernel = matern_block(target_points, source_points)
            values = jnp.take(direction, source, axis=1)
            part = jnp.einsum('lab,nlb->nla', kernel, values, precision=highest)
            keep = (slot_index < block_counts).astype(jnp.float32)
            return (total + part * keep[None, :, None], None)
        total, unused = lax.scan(one_slot, jnp.zeros((PROBES, width, LEAF_SIZE), jnp.float32), jnp.arange(NEAR_SLOTS, dtype=jnp.int32))
        return total
    result = lax.map(one_block, (point_blocks, id_blocks, count_blocks))
    return result.transpose(1, 0, 2, 3).reshape(PROBES, LEAVES, LEAF_SIZE)

def reference(points, solution, residual, direction, nugget, leaf_basis, transfer, far_coupling, coarse_up, coarse_down, near_ids, near_count, far_ids):
    coefficients = jnp.einsum('nla,lar->nlr', direction, leaf_basis, precision=highest)
    near = near_field(points, direction, near_ids, near_count) + nugget[None] * direction
    far_coeff = jnp.take(coefficients, far_ids.reshape(-1), axis=1).reshape(PROBES, LEAVES, FAR_SLOTS, RANK)
    local_coeff = jnp.einsum('nlfq,lfqr->nlr', far_coeff, far_coupling, precision=highest)
    box_transfer = transfer.reshape(BOXES, LEAF_DEV, RANK, RANK)
    box = jnp.einsum('ndlq,dlqr->ndr', coefficients.reshape(PROBES, BOXES, LEAF_DEV, RANK), box_transfer, precision=highest)
    level = jnp.einsum('ndq,dkqr->kdnr', box, coarse_up, precision=highest)
    down = jnp.zeros((BOXES, PROBES, RANK), jnp.float32)
    for depth in range(LEVELS):
        span = 2 ** depth
        pairs = BOXES // (2 * span)
        sums = level[depth].reshape(pairs, 2, span, PROBES, RANK).sum(axis=2)
        other = sums[:, ::-1]
        sibling = jnp.broadcast_to(other[:, :, None], (pairs, 2, span, PROBES, RANK)).reshape(BOXES, PROBES, RANK)
        down = down + 2.0 ** (-0.5 * depth) * jnp.einsum('dnr,drq->dnq', sibling, coarse_down[:, depth], precision=highest)
    pushed = jnp.einsum('dnq,dlrq->ndlr', down, box_transfer, precision=highest).reshape(PROBES, LEAVES, RANK)
    local_coeff = local_coeff + pushed
    image = near + jnp.einsum('nlr,lar->nla', local_coeff, leaf_basis, precision=highest)
    start = lax.optimization_barrier(jnp.sum(residual * residual, axis=(1, 2)))
    curvature = lax.optimization_barrier(jnp.sum(direction * image, axis=(1, 2)))
    alpha = (start / curvature)[:, None, None]
    new_solution = solution + alpha * direction
    new_residual = residual - alpha * image
    finish = lax.optimization_barrier(jnp.sum(new_residual * new_residual, axis=(1, 2)))
    new_direction = new_residual + (finish / (start + epsilon))[:, None, None] * direction
    return (new_solution, new_residual, new_direction)
```

```python
import functools
import math

import jax
import jax.numpy as jnp
from jax import lax
from jax.experimental import pallas as pl
from jax.experimental.pallas import tpu as pltpu
from jax.sharding import PartitionSpec as P

epsilon = 1e-06
ln2 = math.log(2.0)
log2e = 1.0 / ln2
point_scale = math.sqrt(3.0) * log2e
f32, bf16 = jnp.float32, jnp.bfloat16
MESH = pl.DeviceIdType.MESH
VMEM = pl.BlockSpec(memory_space=pltpu.VMEM)
SMEM = pl.BlockSpec(memory_space=pltpu.SMEM)
ANY = pl.BlockSpec(memory_space=pl.ANY)

LEAF, RANK, PROBES, NEAR, FAR, OWN, LEVELS = 512, 128, 16, 27, 16, 4, 8
SIDE, DEPTH = 4, 8
ROWS = 24
GROUP = OWN * SIDE * SIDE
PEERS = SIDE * SIDE


def split(value):
    high = value.astype(bf16)
    return high, (value - high.astype(f32)).astype(bf16)


def dot3(left, right, dims):
    (lh, ll), (rh, rl) = split(left), split(right)
    dot = functools.partial(lax.dot_general, dimension_numbers=(dims, ((), ())), preferred_element_type=f32)
    return dot(lh, rh) + (dot(ll, rh) + dot(lh, rl))


NN, NT = ((1,), (0,)), ((1,), (1,))


def exchange_kernel(packet, level, gathered, sibling, pending, arrived, send, receive, own_sem, tree_send, tree_receive):
    hi, lo = lax.axis_index("hi"), lax.axis_index("lo")
    x, y = lo // SIDE, lo % SIDE
    z, core = hi // 2, hi % 2

    def at(dx, dy):
        return ((x + dx) % SIDE) * SIDE + (y + dy) % SIDE

    def flip(value, bit):
        return value + (1 << bit) - 2 * (((value // (1 << bit)) % 2) * (1 << bit))

    partners = [(hi, flip(lo, k)) for k in range(4)] + [(flip(hi, k), lo) for k in range(4)]
    barrier = pltpu.get_barrier_semaphore()
    greeted = [(hi, at(0, 1)), (hi, at(0, 3)), (hi, at(0, 2)), (hi, at(1, 0)), (hi, at(3, 0)), (hi, at(2, 0))] + partners[4:]
    for device in greeted:
        pl.semaphore_signal(barrier, inc=1, device_id=device, device_id_type=MESH)
    own = pltpu.make_async_copy(packet, gathered.at[pl.ds(lo * OWN, OWN)], own_sem)
    own.start()
    pl.semaphore_wait(barrier, len(greeted))

    sends = []

    def push(dx, dy, leaf, to, source=None):
        slot = at(dx, dy) * OWN + leaf
        copy = pltpu.make_async_remote_copy(
            src_ref=packet.at[leaf] if (dx, dy) == (0, 0) else gathered.at[slot],
            dst_ref=gathered.at[slot],
            send_sem=send.at[len(sends)],
            recv_sem=receive.at[slot],
            device_id=(hi, at(*to)),
            device_id_type=MESH,
        )
        copy.start()
        sends.append(copy)

    def landed(dx, dy, leaf):
        slot = at(dx, dy) * OWN + leaf
        pltpu.make_async_remote_copy(
            src_ref=gathered.at[slot],
            dst_ref=gathered.at[slot],
            send_sem=send.at[0],
            recv_sem=receive.at[slot],
            device_id=(hi, lo),
            device_id_type=MESH,
        ).wait_recv()

    def turn(first, second, half):
        return (second, first) if half == 0 else (first, second)

    tree = []

    def tree_start(k):
        copy = pltpu.make_async_remote_copy(
            src_ref=(level if k == 0 else pending.at[k, pl.ds(0, LEVELS - k)]),
            dst_ref=arrived.at[k, pl.ds(0, LEVELS - k)],
            send_sem=tree_send.at[k],
            recv_sem=tree_receive.at[k],
            device_id=partners[k],
            device_id_type=MESH,
        )
        copy.start()
        tree.append(copy)

    def tree_finish(k):
        tree[k].wait_recv()
        sibling[k] = arrived[k, 0]
        if k < LEVELS - 1:
            mine = level if k == 0 else pending.at[k]
            pending[k + 1, pl.ds(0, LEVELS - 1 - k)] = mine[pl.ds(1, LEVELS - 1 - k)] + arrived[k, pl.ds(1, LEVELS - 1 - k)]

    tree_start(0)
    for half in (0, 1):
        for leaf in (2 * half, 2 * half + 1):
            for step in (1, 3):
                push(0, 0, leaf, turn(step, 0, half) if half else (0, step))
    for half in (0, 1):
        for leaf in (2 * half, 2 * half + 1):
            for step in (1, 3):
                push(0, 0, leaf, (step, 0) if half == 0 else (0, step))
    tree_finish(0)
    tree_start(1)

    def first(half, step):
        return (0, step) if half == 0 else (step, 0)

    def second(half, step):
        return (step, 0) if half == 0 else (0, step)

    def add(a, b):
        return (a[0] + b[0], a[1] + b[1])

    for half in (0, 1):
        for leaf in (2 * half, 2 * half + 1):
            for step in (3, 1):
                landed(*first(half, step), leaf)
                if (leaf % 2 == 0) == (step == 3):
                    push(*first(half, step), leaf, first(half, 4 - step))
                push(*first(half, step), leaf, second(half, 1))
                push(*first(half, step), leaf, second(half, 3))
    tree_finish(1)
    tree_start(2)
    for half in (0, 1):
        for leaf in (2 * half, 2 * half + 1):
            for step in (3, 1):
                landed(*second(half, step), leaf)
                if (leaf % 2 == 0) == (step == 3):
                    push(*second(half, step), leaf, second(half, 4 - step))
    tree_finish(2)
    tree_start(3)
    for half in (0, 1):
        for leaf in (2 * half, 2 * half + 1):
            landed(*first(half, 2), leaf)
            push(*first(half, 2), leaf, second(half, 1))
            push(*first(half, 2), leaf, second(half, 3))
    tree_finish(3)
    tree_start(4)
    for across in (3, 1, 2):
        for half in (0, 1):
            for leaf in (2 * half, 2 * half + 1):
                for step in (3, 1):
                    where = add(first(half, across), second(half, step))
                    landed(*where, leaf)
                    if (leaf % 2 == 0) == (step == 3):
                        push(*where, leaf, second(half, 4 - step))
        if across == 3:
            tree_finish(4)
            tree_start(5)
        if across == 1:
            tree_finish(5)
            tree_start(6)
    tree_finish(6)
    tree_start(7)
    for across in (0, 3, 1, 2):
        for half in (0, 1):
            for leaf in (2 * half, 2 * half + 1):
                landed(*add(first(half, across), second(half, 2)), leaf)
    tree_finish(7)
    for copy in sends:
        copy.wait_send()
    for copy in tree:
        copy.wait_send()
    own.wait()


def exchange(packet, level):
    return pl.pallas_call(
        exchange_kernel,
        out_shape=(
            jax.ShapeDtypeStruct((GROUP, ROWS, LEAF), f32),
            jax.ShapeDtypeStruct((LEVELS, PROBES, RANK), f32),
        ),
        in_specs=[ANY, VMEM],
        out_specs=(ANY, VMEM),
        scratch_shapes=[
            pltpu.VMEM((LEVELS, LEVELS, PROBES, RANK), f32),
            pltpu.VMEM((LEVELS, LEVELS, PROBES, RANK), f32),
            pltpu.SemaphoreType.DMA((60,)),
            pltpu.SemaphoreType.DMA((GROUP,)),
            pltpu.SemaphoreType.DMA,
            pltpu.SemaphoreType.DMA((LEVELS,)),
            pltpu.SemaphoreType.DMA((LEVELS,)),
        ],
        compiler_params=pltpu.CompilerParams(collective_id=0, has_side_effects=True),
        name="exchange",
    )(packet, level)


def image_kernel(
    ids, counts, far_ids, gathered_hbm, sibling, residual, nugget, basis_hbm, transfer, coupling_hbm, coarse_down_hbm,
    image, stats,
    gathered, basis, coupling, coarse_down, sources, targets, values, total, distance0, distance1, task_leaf, task_source,
    coeff, sems,
):
    hi, lo = lax.axis_index("hi"), lax.axis_index("lo")
    copies = [
        pltpu.make_async_copy(gathered_hbm, gathered, sems.at[0]),
        pltpu.make_async_copy(coarse_down_hbm, coarse_down, sems.at[1]),
        pltpu.make_async_copy(coupling_hbm, coupling, sems.at[2]),
        pltpu.make_async_copy(basis_hbm, basis, sems.at[3]),
    ]
    for copy in copies:
        copy.start()
    total[...] = jnp.zeros_like(total)
    tasks = jnp.int32(0)
    for leaf in range(OWN):
        start = tasks

        @pl.loop(0, counts[leaf])
        def _(slot):
            task_leaf[start + slot] = leaf
            task_source[start + slot] = ids[leaf * NEAR + slot]

        tasks = tasks + counts[leaf]
    for extra in range(2):
        task_leaf[tasks + extra] = OWN
        task_source[tasks + extra] = 0

    def as_float(value):
        return value.astype(f32)

    center = (
        as_float(4 * (hi % 2) + 8 * ((hi // 8) % 2) + 2),
        as_float(4 * ((hi // 2) % 2) + 2),
        as_float(4 * ((hi // 4) % 2) + 2),
    )
    row = lax.broadcasted_iota(jnp.int32, (8, LEAF), 0)
    middle = jnp.where(row == 0, center[0], jnp.where(row == 1, center[1], center[2]))
    copies[0].wait()

    def features(leaf):
        raw = gathered[leaf, 16:24, :]
        moved = jnp.where(row < 3, (raw - middle) * point_scale, 0.0)
        square = jnp.sum(moved * moved, axis=0, keepdims=True)
        return moved, square

    def parts(value):
        high = value.astype(bf16).astype(f32)
        rest = value - high
        mid = rest.astype(bf16).astype(f32)
        return high, mid, rest - mid

    @pl.loop(0, GROUP)
    def _(leaf):
        moved, square = features(leaf)
        high, mid, low = parts(jnp.where(row == 3, square, jnp.where(row == 4, 1.0, moved)))
        sources[leaf] = jnp.concatenate([high, mid, high, mid, low, high], axis=0).astype(bf16)
        vh, vl = split(gathered[leaf, 0:16, :])
        values[leaf] = jnp.concatenate([vh, vl], axis=0)

    for leaf in range(OWN):
        moved, square = features(lo * OWN + leaf)
        high, mid, low = parts(jnp.where(row == 3, 1.0, jnp.where(row == 4, square, -2.0 * moved)))
        targets[leaf] = jnp.concatenate([high, high, mid, mid, high, low], axis=0).astype(bf16)

    def measure(task, into):
        leaf, source = task_leaf[task] % OWN, task_source[task]
        into[...] = lax.dot_general(
            sources[source], targets[leaf], (((0,), (0,)), ((), ())), preferred_element_type=f32
        )

    def apply(task, distance):
        leaf, source = task_leaf[task], task_source[task]
        value = values[source]
        part = jnp.zeros((2 * PROBES, LEAF), f32)
        for at in range(0, LEAF, 128):
            squared = jnp.maximum(distance[at : at + 128], 1e-30)
            scaled = squared * lax.rsqrt(squared)
            kernel = (scaled + log2e) * jnp.exp2(-scaled)
            kh, kl = split(kernel)
            here = value[:, at : at + 128]
            part += jnp.dot(
                jnp.concatenate([here, here], axis=1), jnp.concatenate([kh, kl], axis=0), preferred_element_type=f32
            )
        total[leaf] += part

    measure(0, distance0)

    @pl.loop(0, (tasks + 1) // 2)
    def _(pair):
        measure(2 * pair + 1, distance1)
        apply(2 * pair, distance0)
        measure(2 * pair + 2, distance0)
        apply(2 * pair + 1, distance1)

    copies[1].wait()
    down = jnp.zeros((PROBES, RANK), f32)
    for k in range(LEVELS):
        down += dot3(sibling[k] * 2.0 ** (-0.5 * k), coarse_down[k], NN)
    copies[2].wait()
    copies[3].wait()
    lane = lax.broadcasted_iota(jnp.int32, (PROBES, 128), 1)
    table = jnp.zeros((PROBES, 128), f32)
    for leaf in range(OWN):
        @pl.loop(0, FAR)
        def _(slot):
            source = far_ids[leaf * FAR + slot]
            for block in range(4):
                coeff[slot, 4 * block : 4 * block + 4, :] = gathered[source, 20:24, 128 * block : 128 * block + 128]

        local = dot3(down, transfer[leaf], NT)
        for slot in range(FAR):
            local += dot3(coeff[slot], coupling[leaf, slot], NN)
        direction = gathered[lo * OWN + leaf, 0:16, :]
        near = (total[leaf, 0:16] + total[leaf, 16:32]) * ln2 + nugget[leaf : leaf + 1, :] * direction
        whole = near + dot3(local, basis[leaf], NT)
        image[leaf] = whole
        mine = residual[leaf]
        small = whole * 0.0625
        for column, product in enumerate((mine * mine, direction * whole, mine * whole, small * small)):
            table += jnp.where(lane == column, jnp.sum(product, axis=1, keepdims=True), 0.0)
    stats[...] = table[0:8] + pltpu.roll(table[8:16], 4, 1)


def make_image(ids, counts, far_ids, gathered, sibling, residual, nugget, basis, transfer, coupling, coarse_down):
    return pl.pallas_call(
        image_kernel,
        out_shape=(jax.ShapeDtypeStruct((OWN, PROBES, LEAF), f32), jax.ShapeDtypeStruct((8, 128), f32)),
        in_specs=[SMEM, SMEM, SMEM, ANY, VMEM, VMEM, VMEM, ANY, VMEM, ANY, ANY],
        out_specs=(VMEM, VMEM),
        scratch_shapes=[
            pltpu.VMEM((GROUP, ROWS, LEAF), f32),
            pltpu.VMEM((OWN, LEAF, RANK), f32),
            pltpu.VMEM((OWN, FAR, RANK, RANK), f32),
            pltpu.VMEM((LEVELS, RANK, RANK), f32),
            pltpu.VMEM((GROUP, 48, LEAF), bf16),
            pltpu.VMEM((OWN, 48, LEAF), bf16),
            pltpu.VMEM((GROUP, 2 * PROBES, LEAF), bf16),
            pltpu.VMEM((OWN + 1, 2 * PROBES, LEAF), f32),
            pltpu.VMEM((LEAF, LEAF), f32),
            pltpu.VMEM((LEAF, LEAF), f32),
            pltpu.SMEM((OWN * NEAR + 4,), jnp.int32),
            pltpu.SMEM((OWN * NEAR + 4,), jnp.int32),
            pltpu.VMEM((FAR, PROBES, RANK), f32),
            pltpu.SemaphoreType.DMA((4,)),
        ],
        compiler_params=pltpu.CompilerParams(vmem_limit_bytes=48 * 2**20),
        name="image",
    )(ids, counts, far_ids, gathered, sibling, residual, nugget, basis, transfer, coupling, coarse_down)


def reduce_kernel(stats, scalars, middle, inner, outer, inner_send, inner_receive, outer_send, outer_receive):
    hi, lo = lax.axis_index("hi"), lax.axis_index("lo")
    barrier = pltpu.get_barrier_semaphore()
    near = [(hi, (lo + step) % PEERS) for step in range(1, PEERS)]
    far = [((hi + step) % (2 * DEPTH), lo) for step in range(1, 2 * DEPTH)]
    for device in near + far:
        pl.semaphore_signal(barrier, inc=1, device_id=device, device_id_type=MESH)
    pl.semaphore_wait(barrier, len(near) + len(far))

    def all_sum(source, slots, send, receive, devices):
        copies = []
        for index, device in enumerate(devices):
            copy = pltpu.make_async_remote_copy(
                src_ref=source,
                dst_ref=slots.at[index],
                send_sem=send.at[index],
                recv_sem=receive.at[index],
                device_id=device,
                device_id_type=MESH,
            )
            copy.start()
            copies.append(copy)
        total = source[...]
        for index, copy in enumerate(copies):
            copy.wait_recv()
            total += slots[index]
        return total, copies

    middle[...], first = all_sum(stats, inner, inner_send, inner_receive, near)
    total, second = all_sum(middle, outer, outer_send, outer_receive, far)
    table = jnp.concatenate([total, pltpu.roll(total, 124, 1)], axis=0)
    start, curvature, cross, square = (table[:, q : q + 1] for q in range(4))
    alpha = start / curvature
    finish = start - 2.0 * (alpha * cross) + (alpha * square) * alpha * 256.0
    beta = finish / (start + epsilon)
    lane = lax.broadcasted_iota(jnp.int32, (PROBES, 128), 1)
    scalars[...] = jnp.where(lane == 0, alpha, beta)
    for copy in first + second:
        copy.wait_send()


def reduce_all(stats):
    return pl.pallas_call(
        reduce_kernel,
        out_shape=jax.ShapeDtypeStruct((PROBES, 128), f32),
        in_specs=[VMEM],
        out_specs=VMEM,
        scratch_shapes=[
            pltpu.VMEM((8, 128), f32),
            pltpu.VMEM((PEERS - 1, 8, 128), f32),
            pltpu.VMEM((2 * DEPTH - 1, 8, 128), f32),
            pltpu.SemaphoreType.DMA((PEERS - 1,)),
            pltpu.SemaphoreType.DMA((PEERS - 1,)),
            pltpu.SemaphoreType.DMA((2 * DEPTH - 1,)),
            pltpu.SemaphoreType.DMA((2 * DEPTH - 1,)),
        ],
        compiler_params=pltpu.CompilerParams(collective_id=1, has_side_effects=True),
        name="reduce",
    )(stats)


def per_device(
    points, solution, residual, direction, nugget, leaf_basis, transfer, far_coupling, coarse_up, coarse_down,
    near_ids, near_count, far_ids,
):
    group_start = lax.axis_index("hi") * GROUP
    by_leaf = jnp.swapaxes(direction, 0, 1)
    high = lax.Precision.HIGHEST
    coefficients = jnp.einsum("lna,lar->lnr", by_leaf, leaf_basis, precision=high)
    box = jnp.einsum("lnq,lqr->nr", coefficients, transfer, precision=high)
    level = jnp.einsum("nq,kqr->knr", box, coarse_up[0], precision=high)
    coeff_rows = coefficients.reshape(OWN, 4, 4, RANK).swapaxes(1, 2).reshape(OWN, 4, LEAF)
    packet = jnp.concatenate(
        [by_leaf, jnp.swapaxes(points, 0, 1), jnp.zeros((OWN, 1, LEAF), f32), coeff_rows], axis=1
    )
    gathered, sibling = exchange(packet, level)
    image, stats = make_image(
        (near_ids - group_start).reshape(-1), near_count, (far_ids - group_start).reshape(-1),
        gathered, sibling, jnp.swapaxes(residual, 0, 1), nugget, leaf_basis, transfer, far_coupling, coarse_down[0],
    )
    scalars = reduce_all(stats)
    alpha, beta = scalars[:, 0:1, None], scalars[:, 1:2, None]
    new_solution = solution + alpha * direction
    new_residual = residual - alpha * jnp.swapaxes(image, 0, 1)
    return new_solution, new_residual, new_residual + beta * direction


def solution(mesh):
    vector, leaf = P(None, ("hi", "lo"), None), ("hi", "lo")
    return jax.shard_map(
        per_device,
        mesh=mesh,
        in_specs=(
            vector, vector, vector, vector, P(leaf, None), P(leaf, None, None), P(leaf, None, None),
            P(leaf, None, None, None), P(leaf, None, None, None), P(leaf, None, None, None),
            P(leaf, None), P(leaf), P(leaf, None),
        ),
        out_specs=(vector, vector, vector),
        check_vma=False,
    )
```
